1024 devices in a mesh: pw: 8 (over z_hi, core), band: 128 (over x, z_lo, y).
Axes of the slice: x: 8, y: 8, z: 8 (z_hi: 4, z_lo: 2; z = z_hi * 2 + z_lo), core: 2. Of those that a mesh axis runs over, the one named last changes fastest.
Arguments:
- wavefunctions: float32 [16384, 8192], P('pw', 'band'), may hold values from -6 to 6
- projectors: float32 [16384, 1024], P('pw', 'band'), may hold values from -0.046875 to 0.046875
- coupling: float32 [4, 256, 256], replicated, may hold values from -1.5 to 1.5
- block_type: int32 [4], replicated, may hold values from 0 to 3
Outputs:
- applied: float32 [16384, 8192], P('pw', 'band')
The draws below stay inside these ranges and needn't reach their ends.
All inputs are finite; a program needn't handle non-finite values.
Results may differ from the reference program's by a relative error of at most 0.000071.
Values sent between devices are 32-bit elements; how exact they have to be, the bound alone decides.
No kernel may reach another device: no remote copies, remote signals or barrier semaphores. Data moves between devices by JAX's collectives and lax.ppermute only.
A program may use at most 32 MiB of HBM per device.

```python
import jax
import jax.numpy as jnp
from jax import lax

BLOCK = 256
NBLOCKS = 4
NTYPES = 4
NPROJ = 1024
NPW = 16384
NB = 8192


def set_ends(result, key, smallest, high):
    longest = result.shape.index(max(result.shape))
    spots = []
    for shift in (0, 1):
        where = [jax.random.randint(jax.random.fold_in(key, axis), (), 0, length) for axis, length in enumerate(result.shape)]
        where[longest] = (where[longest] + shift) % result.shape[longest]
        spots.append(tuple(where))
    return result.at[spots[0]].set(smallest).at[spots[1]].set(high)


def block_levels(rng, dims, shards, smallest, largest):
    loudness = 1.0
    for axis_at, blocks in shards:
        steps = jax.random.uniform(jax.random.fold_in(jax.random.fold_in(rng, 6), axis_at), (blocks,), jnp.float32, smallest / len(shards), largest / len(shards))
        loudness = loudness * jnp.repeat(jnp.exp(steps), dims[axis_at] // blocks).reshape((-1,) + (1,) * (len(dims) - 1 - axis_at))
    return loudness


def normal_values(stream_key, dims, spread, limit, cuts=(), dtype=jnp.bfloat16):
    values = spread * jax.random.normal(stream_key, dims, jnp.float32)
    if cuts:
        values = values * block_levels(stream_key, dims, cuts, -0.22, 0.18)
    return jnp.clip(values, -limit, limit).astype(dtype)


def setup_inputs(seed: int = 0) -> dict:
    arg_keys = jax.random.split(jax.random.key(seed), 5)
    wavefunctions = normal_values(arg_keys[0], (NPW, NB), 1.0, 6.0, ((0, 8), (1, 128)), jnp.float32)
    projectors = normal_values(arg_keys[1], (NPW, NPROJ), NPW ** -0.5, 0.046875, ((0, 8), (1, 128)), jnp.float32)
    coupling = normal_values(arg_keys[2], (NTYPES, BLOCK, BLOCK), (BLOCK * NPROJ // NPW) ** -0.5, 1.5, (), jnp.float32)
    block_type = set_ends(jax.random.randint(arg_keys[3], (NBLOCKS,), 0, NTYPES), jax.random.fold_in(arg_keys[3], 1), 0, NTYPES - 1).astype(jnp.int32)
    return {"wavefunctions": wavefunctions, "projectors": projectors, "coupling": coupling, "block_type": block_type}


def reference(wavefunctions, projectors, coupling, block_type):
    projections = lax.dot_general(projectors, wavefunctions, (((0,), (0,)), ((), ())), precision=lax.Precision.HIGHEST, preferred_element_type=jnp.float32)
    blocks = coupling[block_type.astype(jnp.int32)]
    grouped = projections.reshape(NBLOCKS, BLOCK, projections.shape[1])
    coupled = jnp.einsum("cij,cjb->cib", blocks, grouped, precision=lax.Precision.HIGHEST).reshape(NPROJ, projections.shape[1])
    return wavefunctions + jnp.dot(projectors, coupled, precision=lax.Precision.HIGHEST, preferred_element_type=jnp.float32)
```

```python
import jax
import jax.numpy as jnp
from jax import lax
from jax.sharding import PartitionSpec as P

PREC = lax.Precision.HIGH


def dot(a, b, dims):
    return lax.dot_general(
        a, b, (dims, ((), ())), precision=PREC, preferred_element_type=jnp.float32
    )


def exact(a, b, dims):
    return lax.dot_general(
        a,
        b,
        (dims, ((), ())),
        precision=lax.Precision.HIGHEST,
        preferred_element_type=jnp.float32,
    )


def make_local(npw, nband, nx, nzl, ny):
    plane = [
        [x * nzl * ny + z * ny + y for x in range(nx) for y in range(ny)] for z in range(nzl)
    ]
    swap = [(i, i ^ ny) for i in range(nband)]

    def local(wavefunctions, projectors, coupling, block_type):
        types, block, _ = coupling.shape
        nblocks = block_type.shape[0]
        wt = wavefunctions.T
        pt = projectors.T
        bands, rows = wt.shape
        mine = pt.shape[0]
        z_lo = (lax.axis_index("band") // ny) % nzl

        other = lax.ppermute(pt, "band", swap)
        both = jnp.where(
            z_lo == 0, jnp.concatenate([pt, other]), jnp.concatenate([other, pt])
        )
        gathered = lax.all_gather(both, "band", axis=0, axis_index_groups=plane, tiled=True)

        nproj = gathered.shape[0]
        at = jnp.arange(block, dtype=jnp.int32)
        j, y, z, outer = (
            at % mine,
            (at // (nzl * mine)) % ny,
            (at // mine) % nzl,
            at // (nzl * ny * mine),
        )
        source = ((outer * nzl + z) * ny + y) * mine + j
        pick = (source[:, None] == at[None, :]).astype(jnp.float32)
        chosen = []
        for i in range(nblocks):
            v = lax.dynamic_index_in_dim(coupling, block_type[i], 0, keepdims=False)
            v = exact(pick, v, ((1,), (0,)))
            chosen.append(exact(v, pick, ((1,), (1,))))

        part = dot(wt, gathered, ((1,), (1,)))
        split = lax.all_to_all(part.reshape(npw, bands // npw, nproj), "pw", 0, 0)
        proj = jnp.sum(split, axis=0)
        coupled = jnp.concatenate(
            [
                dot(proj[:, i * block : (i + 1) * block], chosen[i], ((1,), (1,)))
                for i in range(nblocks)
            ],
            axis=1,
        )
        full = lax.all_to_all(
            jnp.broadcast_to(coupled[None], (npw,) + coupled.shape), "pw", 0, 0
        ).reshape(bands, nproj)
        out = wt + dot(full, gathered, ((1,), (0,)))
        return out.T

    return local


def solution(mesh):
    npw, nband = mesh.shape["pw"], mesh.shape["band"]
    local = make_local(npw, nband, 8, 2, 8)
    return jax.shard_map(
        local,
        mesh=mesh,
        in_specs=(P("pw", "band"), P("pw", "band"), P(), P()),
        out_specs=P("pw", "band"),
        check_vma=False,
    )
```

```python
import jax
import jax.numpy as jnp
from jax import lax
from jax.sharding import PartitionSpec as P


def dot(a, b, dims, precision=lax.Precision.HIGH):
    return lax.dot_general(
        a, b, (dims, ((), ())), precision=precision, preferred_element_type=jnp.float32
    )


def make_local(npw, nx, nzl, ny):
    nband = nx * nzl * ny

    def at(x, z, y):
        return (x * nzl + z) * ny + y

    along_y = [[at(x, z, y) for y in range(ny)] for x in range(nx) for z in range(nzl)]
    along_x = [[at(x, z, y) for x in range(nx)] for z in range(nzl) for y in range(ny)]
    column = [
        [p * nband + at(x, z, y) for z in range(nzl) for p in range(npw)]
        for x in range(nx)
        for y in range(ny)
    ]
    swap = [(i, i ^ ny) for i in range(nband)]
    both = ("pw", "band")

    def local(wavefunctions, projectors, coupling, block_type):
        block = coupling.shape[1]
        nblocks = block_type.shape[0]
        wt = wavefunctions.T
        pt = projectors.T
        bands, rows = wt.shape
        mine = pt.shape[0]
        first = (lax.axis_index("band") // ny) % nzl == 0
        members = nzl * npw

        line = lax.all_to_all(
            jnp.broadcast_to(pt[None], (ny, mine, rows)), "band", 0, 0, axis_index_groups=along_y
        ).reshape(ny * mine, rows)
        gathered = lax.all_gather(line, "band", axis=0, axis_index_groups=along_x, tiled=True)
        held = gathered.shape[0]

        other = lax.ppermute(wt, "band", swap)
        pair = jnp.where(first, jnp.concatenate([wt, other]), jnp.concatenate([other, wt]))

        piece = block // nzl
        spot = jnp.arange(block, dtype=jnp.int32)
        z, outer, inner = spot // piece, (spot % piece) // (ny * mine), spot % (ny * mine)
        source = (outer * nzl + z) * (ny * mine) + inner
        pick = (source[:, None] == spot[None, :]).astype(jnp.float32)
        mixers = []
        for i in range(nblocks):
            v = lax.dynamic_index_in_dim(coupling, block_type[i], 0, keepdims=False)
            v = dot(pick, v, ((1,), (0,)), lax.Precision.HIGHEST)
            mixers.append(dot(v, pick, ((1,), (1,)), lax.Precision.HIGHEST))

        part = dot(pair, gathered, ((1,), (1,)))
        few = nzl * bands // members
        split = lax.all_to_all(
            part.reshape(members, few, held), both, 0, 0, axis_index_groups=column
        )
        proj = jnp.sum(split.reshape(nzl, npw, few, held), axis=1)
        coupled = []
        for i in range(nblocks):
            own = [proj[z, :, i * piece : (i + 1) * piece] for z in range(nzl)]
            coupled.append(dot(jnp.concatenate(own, axis=1), mixers[i], ((1,), (1,))))
        back = jnp.stack(
            [
                jnp.concatenate([c[:, z * piece : (z + 1) * piece] for c in coupled], axis=1)
                for z in range(nzl)
            ]
        )
        back = jnp.broadcast_to(back[:, None], (nzl, npw, few, held)).reshape(members, few, held)
        full = lax.all_to_all(back, both, 0, 0, axis_index_groups=column).reshape(
            nzl * bands, held
        )
        low, high = full[:bands], full[bands:]
        sent = dot(jnp.where(first, high, low), gathered, ((1,), (0,)))
        received = lax.ppermute(sent, "band", swap)
        kept = wt + dot(jnp.where(first, low, high), gathered, ((1,), (0,)))
        return (lax.optimization_barrier(kept) + received).T

    return local


def solution(mesh):
    nx, nzl, ny = 8, 2, 8
    local = make_local(mesh.shape["pw"], nx, nzl, ny)
    return jax.shard_map(
        local,
        mesh=mesh,
        in_specs=(P("pw", "band"), P("pw", "band"), P(), P()),
        out_specs=P("pw", "band"),
        check_vma=False,
    )
```

```python
import jax
import jax.numpy as jnp
from jax import lax
from jax.sharding import PartitionSpec as P

BOTH = ("pw", "band")
CORES = 2


def dot(a, b, dims, precision=lax.Precision.HIGH):
    return lax.dot_general(
        a, b, (dims, ((), ())), precision=precision, preferred_element_type=jnp.float32
    )


def make_local(npw, nx, nzl, ny):
    side, nband = nx, nx * nzl * ny

    def at(pw, x, z, y):
        return pw * nband + (x * nzl + z) * ny + y

    every = [
        (pw, x, z, y) for pw in range(npw) for x in range(nx) for z in range(nzl) for y in range(ny)
    ]

    def on_x(pw, turn):
        return (pw % CORES == 0) != (turn == 0)

    def lines(turn):
        groups = []
        for pw in range(npw):
            for z in range(nzl):
                for fixed in range(side):
                    if on_x(pw, turn):
                        groups.append([at(pw, i, z, fixed) for i in range(side)])
                    else:
                        groups.append([at(pw, fixed, z, i) for i in range(side)])
        return groups

    def step(turn, by):
        pairs = []
        for pw, x, z, y in every:
            if on_x(pw, turn):
                pairs.append((at(pw, x, z, y), at(pw, (x + by) % nx, z, y)))
            else:
                pairs.append((at(pw, x, z, y), at(pw, x, z, (y + by) % ny)))
        return pairs

    column = [
        [at(pw, x, z, y) for z in range(nzl) for pw in range(npw)]
        for x in range(nx)
        for y in range(ny)
    ]
    swap = [(at(pw, x, z, y), at(pw, x, z ^ 1, y)) for pw, x, z, y in every]
    offsets = [0]
    for hop in range(1, side // 2):
        offsets += [-hop, hop]
    offsets.append(side // 2)

    def ring(blocks, turns):
        up, down = list(blocks), list(blocks)
        kept = [[b] for b in blocks]
        for hop in range(side // 2):
            last = hop == side // 2 - 1
            if last:
                rows = up[0].shape[0] // 2
                up = [u[:rows] for u in up]
                down = [d[rows:] for d in down]
            up = [lax.ppermute(u, BOTH, step(t, 1)) for u, t in zip(up, turns)]
            down = [lax.ppermute(d, BOTH, step(t, -1)) for d, t in zip(down, turns)]
            for k, u, d in zip(kept, up, down):
                k += [jnp.concatenate([u, d])] if last else [u, d]
        return [jnp.concatenate(k) for k in kept]

    def local(wavefunctions, projectors, coupling, block_type):
        block = coupling.shape[1]
        nblocks = block_type.shape[0]
        wt = wavefunctions.T
        pt = projectors.T
        bands, rows = wt.shape
        mine = pt.shape[0]
        place = lax.axis_index("band")
        first = (place // ny) % nzl == 0
        my_x, my_y = place // (nzl * ny), place % ny
        core = lax.axis_index("pw") % CORES
        members = nzl * npw
        half = rows // 2
        held = side * side * mine

        starts = []
        for h in range(2):
            piece = pt[:, h * half : (h + 1) * half]
            starts.append(
                lax.all_to_all(
                    jnp.broadcast_to(piece[None], (side, mine, half)),
                    BOTH,
                    0,
                    0,
                    axis_index_groups=lines(h),
                ).reshape(side * mine, half)
            )
        other = lax.ppermute(wt, BOTH, swap)
        halves = ring(starts, (1, 0))
        pair = jnp.where(first, jnp.concatenate([wt, other]), jnp.concatenate([other, wt]))

        spot = jnp.arange(held, dtype=jnp.int32)
        outer, inner, j = spot // (side * mine), (spot // mine) % side, spot % mine
        shift = jnp.zeros_like(spot)
        for i, o in enumerate(offsets):
            shift = jnp.where(outer == i, o % side, shift)
        places = []
        for h in range(2):
            x_last = (core == 0) == (h == 0)
            ring_at = (jnp.where(x_last, my_x, my_y) + shift) % side
            x = jnp.where(x_last, ring_at, inner)
            y = jnp.where(x_last, inner, ring_at)
            places.append((x * side + y) * mine + j)
        order = (jnp.concatenate(places)[:, None] == spot[None, :]).astype(jnp.float32)

        piece = block // nzl
        b_at = jnp.arange(block, dtype=jnp.int32)
        z, out_at, in_at = b_at // piece, (b_at % piece) // (ny * mine), b_at % (ny * mine)
        source = (out_at * nzl + z) * (ny * mine) + in_at
        pick = (source[:, None] == b_at[None, :]).astype(jnp.float32)
        mixers = []
        for i in range(nblocks):
            v = lax.dynamic_index_in_dim(coupling, block_type[i], 0, keepdims=False)
            v = dot(pick, v, ((1,), (0,)), lax.Precision.HIGHEST)
            mixers.append(dot(v, pick, ((1,), (1,)), lax.Precision.HIGHEST))

        parts = [
            dot(pair[:, h * half : (h + 1) * half], halves[h], ((1,), (1,))) for h in range(2)
        ]
        part = dot(jnp.concatenate(parts, axis=1), order, ((1,), (0,)), lax.Precision.HIGHEST)
        few = nzl * bands // members
        split = lax.all_to_all(
            part.reshape(members, few, held), BOTH, 0, 0, axis_index_groups=column
        )
        proj = jnp.sum(split.reshape(nzl, npw, few, held), axis=1)
        coupled = []
        for i in range(nblocks):
            own = [proj[z, :, i * piece : (i + 1) * piece] for z in range(nzl)]
            coupled.append(dot(jnp.concatenate(own, axis=1), mixers[i], ((1,), (1,))))
        back = jnp.stack(
            [
                jnp.concatenate([c[:, z * piece : (z + 1) * piece] for c in coupled], axis=1)
                for z in range(nzl)
            ]
        )
        back = jnp.broadcast_to(back[:, None], (nzl, npw, few, held)).reshape(members, few, held)
        full = lax.all_to_all(back, BOTH, 0, 0, axis_index_groups=column).reshape(
            nzl * bands, held
        )
        full = dot(full, order, ((1,), (1,)), lax.Precision.HIGHEST)
        low, high = full[:bands], full[bands:]

        def apply(d):
            return jnp.concatenate(
                [dot(d[:, h * held : (h + 1) * held], halves[h], ((1,), (0,))) for h in range(2)],
                axis=1,
            )

        sent = apply(jnp.where(first, high, low))
        received = lax.ppermute(sent, BOTH, swap)
        kept = wt + apply(jnp.where(first, low, high))
        return (lax.optimization_barrier(kept) + received).T

    return local


def solution(mesh):
    local = make_local(mesh.shape["pw"], 8, 2, 8)
    return jax.shard_map(
        local,
        mesh=mesh,
        in_specs=(P("pw", "band"), P("pw", "band"), P(), P()),
        out_specs=P("pw", "band"),
        check_vma=False,
    )
```

```python
import jax
import jax.numpy as jnp
from jax import lax
from jax.sharding import PartitionSpec as P


def dot(a, b, dims, precision=lax.Precision.HIGH):
    return lax.dot_general(
        a, b, (dims, ((), ())), precision=precision, preferred_element_type=jnp.float32
    )


def make_local(npw, nx, nzl, ny):
    nband = nx * nzl * ny
    both = ("pw", "band")

    def at(x, z, y):
        return (x * nzl + z) * ny + y

    spots = [(x, z, y) for x in range(nx) for z in range(nzl) for y in range(ny)]
    along_y = [[at(x, z, y) for y in range(ny)] for x in range(nx) for z in range(nzl)]
    along_x = [[at(x, z, y) for x in range(nx)] for z in range(nzl) for y in range(ny)]
    column = [
        [p * nband + at(x, z, y) for z in range(nzl) for p in range(npw)]
        for x in range(nx)
        for y in range(ny)
    ]
    swap = [(at(x, z, y), at(x, z ^ 1, y)) for x, z, y in spots]

    def step(by):
        return [(at(x, z, y), at(x, z, (y + by) % ny)) for x, z, y in spots]

    def line(piece, groups, side):
        mine, half = piece.shape
        spread = jnp.broadcast_to(piece[None], (side, mine, half))
        return lax.all_to_all(spread, "band", 0, 0, axis_index_groups=groups)

    def ring(block, my_y):
        shape = (nx, ny) + block.shape[2:]

        def put(whole, part, y, x):
            return lax.dynamic_update_slice(whole, part, (x, y % ny, 0, 0))

        whole = put(jnp.zeros(shape, block.dtype), block, my_y, 0)
        up = down = block
        for hop in range(1, ny // 2):
            up = lax.ppermute(up, "band", step(1))
            down = lax.ppermute(down, "band", step(-1))
            whole = put(whole, up, my_y - hop + ny, 0)
            whole = put(whole, down, my_y + hop, 0)
        up = lax.ppermute(up[: nx // 2], "band", step(1))
        down = lax.ppermute(down[nx // 2 :], "band", step(-1))
        whole = put(whole, up, my_y + ny // 2, 0)
        return put(whole, down, my_y + ny // 2, nx // 2)

    def local(wavefunctions, projectors, coupling, block_type):
        block = coupling.shape[1]
        nblocks = block_type.shape[0]
        wt = wavefunctions.T
        pt = projectors.T
        bands, rows = wt.shape
        mine = pt.shape[0]
        place = lax.axis_index("band")
        first = (place // ny) % nzl == 0
        my_y = place % ny
        members = nzl * npw
        half = rows // 2
        held = nx * ny * mine

        line_a = line(pt[:, :half], along_y, ny).reshape(ny * mine, half)
        gathered_a = lax.all_gather(line_a, "band", axis=0, axis_index_groups=along_x, tiled=True)
        line_a, piece_b, wt_out = lax.optimization_barrier((line_a, pt[:, half:], wt))
        other = lax.ppermute(wt_out, "band", swap)
        line_b = line(piece_b, along_x, nx).reshape(nx, 1, mine, half)
        gathered_b = ring(line_b, my_y).reshape(held, half)
        pair = jnp.where(first, jnp.concatenate([wt, other]), jnp.concatenate([other, wt]))

        piece = block // nzl
        spot = jnp.arange(block, dtype=jnp.int32)
        z, outer, inner = spot // piece, (spot % piece) // (ny * mine), spot % (ny * mine)
        source = (outer * nzl + z) * (ny * mine) + inner
        pick = (source[:, None] == spot[None, :]).astype(jnp.float32)
        mixers = []
        for i in range(nblocks):
            v = lax.dynamic_index_in_dim(coupling, block_type[i], 0, keepdims=False)
            v = dot(pick, v, ((1,), (0,)), lax.Precision.HIGHEST)
            mixers.append(dot(v, pick, ((1,), (1,)), lax.Precision.HIGHEST))
        pair, *mixers = lax.optimization_barrier((pair, *mixers))

        part_b = lax.optimization_barrier(dot(pair[:, half:], gathered_b, ((1,), (1,))))
        part = part_b + dot(pair[:, :half], gathered_a, ((1,), (1,)))
        few = nzl * bands // members
        split = lax.all_to_all(
            part.reshape(members, few, held), both, 0, 0, axis_index_groups=column
        )
        proj = jnp.sum(split.reshape(nzl, npw, few, held), axis=1)
        coupled = []
        for i in range(nblocks):
            own = [proj[z, :, i * piece : (i + 1) * piece] for z in range(nzl)]
            coupled.append(dot(jnp.concatenate(own, axis=1), mixers[i], ((1,), (1,))))
        back = jnp.stack(
            [
                jnp.concatenate([c[:, z * piece : (z + 1) * piece] for c in coupled], axis=1)
                for z in range(nzl)
            ]
        )
        back = jnp.broadcast_to(back[:, None], (nzl, npw, few, held)).reshape(members, few, held)
        full = lax.all_to_all(back, both, 0, 0, axis_index_groups=column).reshape(
            nzl * bands, held
        )
        low, high = full[:bands], full[bands:]
        away, home = jnp.where(first, high, low), jnp.where(first, low, high)
        received = [
            lax.ppermute(dot(away, g, ((1,), (0,))), "band", swap)
            for g in (gathered_a, gathered_b)
        ]
        kept = [
            wt[:, :half] + dot(home, gathered_a, ((1,), (0,))),
            wt[:, half:] + dot(home, gathered_b, ((1,), (0,))),
        ]
        kept = lax.optimization_barrier(kept)
        return jnp.concatenate([k + r for k, r in zip(kept, received)], axis=1).T

    return local


def solution(mesh):
    local = make_local(mesh.shape["pw"], 8, 2, 8)
    return jax.shard_map(
        local,
        mesh=mesh,
        in_specs=(P("pw", "band"), P("pw", "band"), P(), P()),
        out_specs=P("pw", "band"),
        check_vma=False,
    )
```

```python
import jax
import jax.numpy as jnp
from jax import lax
from jax.sharding import PartitionSpec as P

BOTH = ("pw", "band")
CORES = 2


def dot(a, b, dims, precision=lax.Precision.HIGH):
    return lax.dot_general(
        a, b, (dims, ((), ())), precision=precision, preferred_element_type=jnp.float32
    )


def make_local(npw, nx, nzl, ny):
    side, nband = nx, nx * nzl * ny

    def at(pw, x, z, y):
        return pw * nband + (x * nzl + z) * ny + y

    def lines(last):
        groups = []
        for pw in range(npw):
            along_x = (pw % CORES == 0) == last
            for z in range(nzl):
                for fixed in range(side):
                    groups.append(
                        [at(pw, i, z, fixed) if along_x else at(pw, fixed, z, i) for i in range(side)]
                    )
        return groups

    column = [
        [at(pw, x, z, y) for z in range(nzl) for pw in range(npw)]
        for x in range(nx)
        for y in range(ny)
    ]
    swap = [
        (at(pw, x, z, y), at(pw, x, z ^ 1, y))
        for pw in range(npw)
        for x in range(nx)
        for z in range(nzl)
        for y in range(ny)
    ]

    def gather(piece, last):
        spread = jnp.broadcast_to(piece[None], (side,) + piece.shape)
        got = lax.all_to_all(spread, BOTH, 0, 0, axis_index_groups=lines(last))
        return got.reshape(side * piece.shape[0], piece.shape[1])

    def local(wavefunctions, projectors, coupling, block_type):
        block = coupling.shape[1]
        nblocks = block_type.shape[0]
        wt = wavefunctions.T
        pt = projectors.T
        bands, rows = wt.shape
        mine = pt.shape[0]
        place = lax.axis_index("band")
        first = (place // ny) % nzl == 0
        core = lax.axis_index("pw") % CORES
        members = nzl * npw
        half = rows // 2
        held = side * side * mine

        line = gather(pt, False)
        gathered = gather(line, True)
        _, wt_out = lax.optimization_barrier((line, wt))
        other = lax.ppermute(wt_out, BOTH, swap)
        pair = jnp.where(first, jnp.concatenate([wt, other]), jnp.concatenate([other, wt]))

        spot = jnp.arange(held, dtype=jnp.int32)
        outer, inner, j = spot // (side * mine), (spot // mine) % side, spot % mine
        shared = jnp.where(core == 0, spot, (inner * side + outer) * mine + j)
        order = (shared[:, None] == spot[None, :]).astype(jnp.float32)

        piece = block // nzl
        b_at = jnp.arange(block, dtype=jnp.int32)
        z, out_at, in_at = b_at // piece, (b_at % piece) // (ny * mine), b_at % (ny * mine)
        source = (out_at * nzl + z) * (ny * mine) + in_at
        pick = (source[:, None] == b_at[None, :]).astype(jnp.float32)
        mixers = []
        for i in range(nblocks):
            v = lax.dynamic_index_in_dim(coupling, block_type[i], 0, keepdims=False)
            v = dot(pick, v, ((1,), (0,)), lax.Precision.HIGHEST)
            mixers.append(dot(v, pick, ((1,), (1,)), lax.Precision.HIGHEST))
        pair, *mixers = lax.optimization_barrier((pair, *mixers))

        part = dot(pair, gathered, ((1,), (1,)))
        part = dot(part, order, ((1,), (0,)), lax.Precision.HIGHEST)
        few = nzl * bands // members
        split = lax.all_to_all(
            part.reshape(members, few, held), BOTH, 0, 0, axis_index_groups=column
        )
        proj = jnp.sum(split.reshape(nzl, npw, few, held), axis=1)
        coupled = []
        for i in range(nblocks):
            own = [proj[z, :, i * piece : (i + 1) * piece] for z in range(nzl)]
            coupled.append(dot(jnp.concatenate(own, axis=1), mixers[i], ((1,), (1,))))
        back = jnp.stack(
            [
                jnp.concatenate([c[:, z * piece : (z + 1) * piece] for c in coupled], axis=1)
                for z in range(nzl)
            ]
        )
        back = jnp.broadcast_to(back[:, None], (nzl, npw, few, held)).reshape(members, few, held)
        full = lax.all_to_all(back, BOTH, 0, 0, axis_index_groups=column).reshape(
            nzl * bands, held
        )
        full = dot(full, order, ((1,), (1,)), lax.Precision.HIGHEST)
        low, high = full[:bands], full[bands:]
        away, home = jnp.where(first, high, low), jnp.where(first, low, high)
        cuts = [gathered[:, :half], gathered[:, half:]]
        received = [lax.ppermute(dot(away, g, ((1,), (0,))), BOTH, swap) for g in cuts]
        kept = [
            wt[:, h * half : (h + 1) * half] + dot(home, g, ((1,), (0,)))
            for h, g in enumerate(cuts)
        ]
        kept = lax.optimization_barrier(kept)
        return jnp.concatenate([k + r for k, r in zip(kept, received)], axis=1).T

    return local


def solution(mesh):
    local = make_local(mesh.shape["pw"], 8, 2, 8)
    return jax.shard_map(
        local,
        mesh=mesh,
        in_specs=(P("pw", "band"), P("pw", "band"), P(), P()),
        out_specs=P("pw", "band"),
        check_vma=False,
    )
```

```python
import jax
import jax.numpy as jnp
from jax import lax
from jax.sharding import PartitionSpec as P

BOTH = ("pw", "band")
CORES = 2


def dot(a, b, dims, precision=lax.Precision.HIGH):
    return lax.dot_general(
        a, b, (dims, ((), ())), precision=precision, preferred_element_type=jnp.float32
    )


def make_local(npw, nx, nzl, ny):
    side, nband = nx, nx * nzl * ny

    def at(pw, x, z, y):
        return pw * nband + (x * nzl + z) * ny + y

    def along_x(pw, last):
        return (pw % CORES == 0) == last

    def lines(last):
        groups = []
        for pw in range(npw):
            for z in range(nzl):
                for fixed in range(side):
                    groups.append(
                        [
                            at(pw, i, z, fixed) if along_x(pw, last) else at(pw, fixed, z, i)
                            for i in range(side)
                        ]
                    )
        return groups

    def step(by):
        pairs = []
        for pw in range(npw):
            for x in range(nx):
                for z in range(nzl):
                    for y in range(ny):
                        to_x, to_y = (by, 0) if along_x(pw, True) else (0, by)
                        to = at(pw, (x + to_x) % nx, z, (y + to_y) % ny)
                        pairs.append((at(pw, x, z, y), to))
        return pairs

    column = [
        [at(pw, x, z, y) for z in range(nzl) for pw in range(npw)]
        for x in range(nx)
        for y in range(ny)
    ]
    swap = [
        (at(pw, x, z, y), at(pw, x, z ^ 1, y))
        for pw in range(npw)
        for x in range(nx)
        for z in range(nzl)
        for y in range(ny)
    ]

    offsets = [0]
    for hop in range(1, side // 2):
        offsets += [-hop, hop]
    offsets.append(side // 2)

    def gather(piece):
        spread = jnp.broadcast_to(piece[None], (side,) + piece.shape)
        got = lax.all_to_all(spread, BOTH, 0, 0, axis_index_groups=lines(False))
        return got.reshape(side * piece.shape[0], piece.shape[1])

    def ring(block):
        up = down = block
        blocks = [block]
        for _ in range(1, side // 2):
            up = lax.ppermute(up, BOTH, step(1))
            down = lax.ppermute(down, BOTH, step(-1))
            blocks += [up, down]
        cut = block.shape[0] // 2
        up = lax.ppermute(up[:cut], BOTH, step(1))
        down = lax.ppermute(down[cut:], BOTH, step(-1))
        return blocks + [jnp.concatenate([up, down])]

    def local(wavefunctions, projectors, coupling, block_type):
        block = coupling.shape[1]
        nblocks = block_type.shape[0]
        wt = wavefunctions.T
        pt = projectors.T
        bands, rows = wt.shape
        mine = pt.shape[0]
        place = lax.axis_index("band")
        first = (place // ny) % nzl == 0
        core = lax.axis_index("pw") % CORES
        members = nzl * npw
        half = rows // 2
        held = side * side * mine

        line = gather(pt)
        blocks = ring(line)
        _, wt_out = lax.optimization_barrier((line, wt))
        other = lax.ppermute(wt_out, BOTH, swap)
        pair = jnp.where(first, jnp.concatenate([wt, other]), jnp.concatenate([other, wt]))

        my_x, my_y = place // (nzl * ny), place % ny
        spot = jnp.arange(held, dtype=jnp.int32)
        outer, inner, j = spot // (side * mine), (spot // mine) % side, spot % mine
        shift = jnp.zeros_like(spot)
        for i, offset in enumerate(offsets):
            shift = jnp.where(outer == i, offset % side, shift)
        around = (jnp.where(core == 0, my_x, my_y) + shift) % side
        x, y = jnp.where(core == 0, around, inner), jnp.where(core == 0, inner, around)
        shared = (x * side + y) * mine + j
        order = (shared[:, None] == spot[None, :]).astype(jnp.float32)

        piece = block // nzl
        b_at = jnp.arange(block, dtype=jnp.int32)
        z, out_at, in_at = b_at // piece, (b_at % piece) // (ny * mine), b_at % (ny * mine)
        source = (out_at * nzl + z) * (ny * mine) + in_at
        pick = (source[:, None] == b_at[None, :]).astype(jnp.float32)
        mixers = []
        for i in range(nblocks):
            v = lax.dynamic_index_in_dim(coupling, block_type[i], 0, keepdims=False)
            v = dot(pick, v, ((1,), (0,)), lax.Precision.HIGHEST)
            mixers.append(dot(v, pick, ((1,), (1,)), lax.Precision.HIGHEST))
        pair, *mixers = lax.optimization_barrier((pair, *mixers))

        part = jnp.concatenate([dot(pair, b, ((1,), (1,))) for b in blocks], axis=1)
        part = dot(part, order, ((1,), (0,)), lax.Precision.HIGHEST)
        blocks, part = lax.optimization_barrier((blocks, part))
        few = nzl * bands // members
        split = lax.all_to_all(
            part.reshape(members, few, held), BOTH, 0, 0, axis_index_groups=column
        )
        proj = jnp.sum(split.reshape(nzl, npw, few, held), axis=1)
        coupled = []
        for i in range(nblocks):
            own = [proj[z, :, i * piece : (i + 1) * piece] for z in range(nzl)]
            coupled.append(dot(jnp.concatenate(own, axis=1), mixers[i], ((1,), (1,))))
        back = jnp.stack(
            [
                jnp.concatenate([c[:, z * piece : (z + 1) * piece] for c in coupled], axis=1)
                for z in range(nzl)
            ]
        )
        back = jnp.broadcast_to(back[:, None], (nzl, npw, few, held)).reshape(members, few, held)
        full = lax.all_to_all(back, BOTH, 0, 0, axis_index_groups=column).reshape(
            nzl * bands, held
        )
        full = dot(full, order, ((1,), (1,)), lax.Precision.HIGHEST)
        low, high = full[:bands], full[bands:]
        away, home = jnp.where(first, high, low), jnp.where(first, low, high)
        cuts = [
            jnp.concatenate([b[:, h * half : (h + 1) * half] for b in blocks]) for h in range(2)
        ]
        cuts = lax.optimization_barrier(cuts)
        received = []
        for g in cuts:
            sent = dot(away, g, ((1,), (0,)))
            sent, away, home = lax.optimization_barrier((sent, away, home))
            received.append(lax.ppermute(sent, BOTH, swap))
        kept = [
            wt[:, h * half : (h + 1) * half] + dot(home, g, ((1,), (0,)))
            for h, g in enumerate(cuts)
        ]
        kept = lax.optimization_barrier(kept)
        return jnp.concatenate([k + r for k, r in zip(kept, received)], axis=1).T

    return local


def solution(mesh):
    local = make_local(mesh.shape["pw"], 8, 2, 8)
    return jax.shard_map(
        local,
        mesh=mesh,
        in_specs=(P("pw", "band"), P("pw", "band"), P(), P()),
        out_specs=P("pw", "band"),
        check_vma=False,
    )
```
